32 devices in a mesh: lat: 4 (over y, x), lon: 8 (over z, core).
Axes of the slice: x: 2, y: 2, z: 4, core: 2. Of those that a mesh axis runs over, the one named last changes fastest.
Arguments:
- adjoint_u: float32 [512, 8192], P('lat', 'lon'), may hold values from -6 to 6
- adjoint_v: float32 [512, 8192], P('lat', 'lon'), may hold values from -6 to 6
- adjoint_h: float32 [512, 8192], P('lat', 'lon'), may hold values from -6 to 6
- zonal_wind: bfloat16 [512, 8192], P('lat', 'lon'), may hold values from -4 to 4
- meridional_wind: bfloat16 [512, 8192], P('lat', 'lon'), may hold values from -4 to 4
- block_inverse: float32 [32, 4096, 256], P('lat', 'lon'), may hold values from -1 to 1
- coupling: float32 [32], P('lat'), may hold values from 0.85 to 1
Outputs:
- out_u: float32 [512, 8192], P('lat', 'lon')
- out_v: float32 [512, 8192], P('lat', 'lon')
- out_h: float32 [512, 8192], P('lat', 'lon')
The draws below stay inside these ranges and needn't reach their ends.
All inputs are finite; a program needn't handle non-finite values.
Results may differ from the reference program's by a relative error of at most 0.0003.
Values sent between devices are 32-bit elements; how exact they have to be, the bound alone decides.
No kernel may reach another device: no remote copies, remote signals or barrier semaphores. Data moves between devices by JAX's collectives and lax.ppermute only.
A program may use at most 128 MiB of HBM per device.

```python
import math
import jax
import jax.numpy as jnp
from jax import lax

NLON = 8192
P_SIZE = 16
NLAT = 512
K = 4096
NBLK = 32


def draw_block_inverse(key, part):
    subkeys = jax.random.split(jax.random.fold_in(key, 11), 6)
    array_shape = (NBLK, K, P_SIZE, P_SIZE)
    identity = jnp.eye(P_SIZE, dtype=jnp.float32)[None, None, :, :]
    diagonal = jax.random.uniform(subkeys[0], (NBLK, K, P_SIZE, 1), jnp.float32, 0.4, 0.8)
    off_diagonal = jax.random.truncated_normal(subkeys[1], -4.0, 4.0, array_shape, jnp.float32) * (0.5 / math.sqrt(P_SIZE))
    slow_modes = jax.random.bernoulli(subkeys[3], 0.5, (K,))
    fast_rate = jax.random.uniform(subkeys[2], (K,), jnp.float32, 0.2, 0.5)
    slow_rate = jax.random.uniform(jax.random.fold_in(subkeys[2], 3), (K,), jnp.float32, 0.965, 0.98)
    carry_rate = jnp.where(slow_modes, slow_rate, fast_rate)
    sign_low = jnp.where(jax.random.bernoulli(subkeys[4], 0.5, (NBLK, K)), 1.0, -1.0).astype(jnp.float32)
    sign_high = jnp.where(jax.random.bernoulli(subkeys[5], 0.5, (NBLK, K)), 1.0, -1.0).astype(jnp.float32)
    blocks = identity * diagonal + (1.0 - identity) * off_diagonal
    blocks = blocks.at[:, :, P_SIZE - 1, 0].set(sign_low * carry_rate[None, :])
    blocks = blocks.at[:, :, 0, P_SIZE - 1].set(sign_high * carry_rate[None, :])
    return blocks.reshape(NBLK, K, P_SIZE * P_SIZE)


def block_scale(key, dims, cuts, least, top_value):
    gain, own = 1.0, jax.random.fold_in(key, 6)
    for position, shards_of in cuts:
        draws = jnp.exp(jax.random.uniform(jax.random.fold_in(own, position), (shards_of,), jnp.float32, least / len(cuts), top_value / len(cuts)))
        gain = gain * jnp.repeat(draws, dims[position] // shards_of).reshape([-1 if axis == position else 1 for axis in range(len(dims))])
    return gain


def normal_values(key, dims, spread, bound, cuts=(), kind=jnp.bfloat16):
    drawn = spread * jax.random.normal(key, dims, jnp.float32)
    if cuts:
        drawn = drawn * block_scale(key, dims, cuts, -0.22, 0.18)
    return jnp.clip(drawn, -bound, bound).astype(kind)


def setup_inputs(seed: int = 0) -> dict:
    seeds = jax.random.split(jax.random.key(seed), 8)
    return {
        "adjoint_u": normal_values(seeds[0], (NLAT, NLON), 1.0, 6.0, ((0, 4), (1, 8)), jnp.float32),
        "adjoint_v": normal_values(seeds[1], (NLAT, NLON), 1.0, 6.0, ((0, 4), (1, 8)), jnp.float32),
        "adjoint_h": normal_values(seeds[2], (NLAT, NLON), 1.0, 6.0, ((0, 4), (1, 8)), jnp.float32),
        "zonal_wind": normal_values(seeds[3], (NLAT, NLON), 1.0, 4.0, ((0, 4), (1, 8))),
        "meridional_wind": normal_values(seeds[4], (NLAT, NLON), 1.0, 4.0, ((0, 4), (1, 8))),
        "block_inverse": draw_block_inverse(jax.random.fold_in(seeds[7], 71), 0),
        "coupling": jnp.clip(0.85 + 0.14999998 * jax.random.uniform(seeds[6], (NBLK,), jnp.float32) ** block_scale(seeds[6], (NBLK,), ((0, 4),), -0.2, 0.2), 0.85, 1.0),
    }


meridional_rate = 0.25


def reference(adjoint_u, adjoint_v, adjoint_h, zonal_wind, meridional_wind, block_inverse, coupling):
    lat_total, lon_count = adjoint_h.shape
    row_index = jnp.arange(lat_total, dtype=jnp.int32).astype(jnp.float32)
    latitude = jnp.pi * (row_index + 0.5) / lat_total - 0.5 * jnp.pi
    stretch = 0.25 / (0.3 + jnp.cos(latitude))
    coriolis = 0.5 * jnp.sin(latitude)
    fields = jnp.stack([adjoint_u, adjoint_v, adjoint_h])
    zonal_flux = zonal_wind.astype(jnp.float32)[None] * fields
    meridional_flux = meridional_wind.astype(jnp.float32)[None] * fields
    result = fields - stretch[None, :, None] * (jnp.roll(zonal_flux, 1, axis=2) - jnp.roll(zonal_flux, -1, axis=2))
    meridional_pad = jnp.pad(meridional_flux, ((0, 0), (1, 1), (0, 0)))
    result = result - meridional_rate * (meridional_pad[:, :-2] - meridional_pad[:, 2:])
    adj_u = result[0] - coriolis[:, None] * adjoint_v
    adj_v = result[1] + coriolis[:, None] * adjoint_u
    adj_h = result[2]
    mode_count = lon_count // 2
    transform = jnp.fft.rfft(adj_h, axis=1)[:, :mode_count]
    wavenumbers = jnp.arange(mode_count, dtype=jnp.int32)
    weight = jnp.where(wavenumbers == 0, 1.0 / lon_count, 2.0 / lon_count).astype(jnp.float32)
    spectrum = jnp.stack([weight * jnp.real(transform), -weight * jnp.imag(transform)], axis=-1)
    blocks = block_inverse.shape[0]
    block_rows = P_SIZE
    inverses = block_inverse.reshape(blocks, mode_count, block_rows, block_rows)
    right_side = spectrum.reshape(blocks, block_rows, mode_count, 2)

    def advance_down(carried, inputs):
        inverse_block, values, coupling_value = inputs
        values = values.at[0].add(-coupling_value * carried)
        product = jnp.einsum('mpq,qmc->pmc', inverse_block, values, precision=lax.Precision.HIGHEST)
        return product[-1], product

    start_state = jnp.zeros((mode_count, 2), jnp.float32)
    _, images = lax.scan(advance_down, start_state, (inverses, right_side, coupling))

    def advance_up(carried, inputs):
        inverse_block, values, coupling_value = inputs
        solved = values - jnp.einsum('mp,mc->pmc', inverse_block[:, :, -1], carried, precision=lax.Precision.HIGHEST)
        return coupling_value * solved[0], solved

    _, solved = lax.scan(advance_up, start_state, (inverses, images, coupling), reverse=True)
    solved = solved.reshape(lat_total, mode_count, 2)
    slope_factor = (2.0 * math.pi / lon_count) * wavenumbers.astype(jnp.float32)
    slope = jnp.stack([slope_factor * solved[..., 1], -slope_factor * solved[..., 0]], axis=-1)
    weights = jnp.where(wavenumbers == 0, 1.0 * lon_count, 0.5 * lon_count).astype(jnp.float32)

    def to_grid(values):
        complex_modes = (values[..., 0] - 1j * values[..., 1]) * weights
        complex_modes = jnp.pad(complex_modes, ((0, 0), (0, 1)))
        return jnp.fft.irfft(complex_modes, n=lon_count, axis=1)

    out_h = to_grid(solved)
    gradient = to_grid(slope)
    out_u = adj_u + stretch[:, None] * gradient
    return out_u, adj_v, out_h
```

```python
import functools
import math

import jax
import jax.numpy as jnp
import numpy as np
from jax import lax
from jax.experimental import pallas as pl
from jax.experimental.pallas import tpu as pltpu
from jax.sharding import PartitionSpec as P

P_SIZE = 16


meridional_rate = 0.25


def padded(cells, sides, width, closed):
    for axis, dim in sides:
        count = lax.axis_size(axis)
        ends = count if closed else count - 1
        head = lax.slice_in_dim(cells, 0, width, axis=dim)
        tail = lax.slice_in_dim(cells, cells.shape[dim] - width, cells.shape[dim], axis=dim)
        cells = jnp.concatenate(
            [
                lax.ppermute(tail, axis, [(i, (i + 1) % count) for i in range(ends)]),
                cells,
                lax.ppermute(head, axis, [((i + 1) % count, i) for i in range(ends)]),
            ],
            axis=dim,
        )
    return cells


def entering(value, axis, combine, identity, reverse):
    peers, mine = (lax.axis_size(axis), lax.axis_index(axis))
    everything = jax.tree.map(lambda part: lax.all_gather(part, axis), value)
    start = jax.tree.map(
        lambda part, zero: jnp.broadcast_to(jnp.asarray(zero, part.dtype), part.shape),
        value,
        identity,
    )

    def lap(k, before):
        at = peers - 1 - k if reverse else k
        reached = at > mine if reverse else at < mine
        new = combine(before, jax.tree.map(lambda part: part[at], everything))
        return jax.tree.map(lambda a, b: jnp.where(reached, a, b), new, before)

    return lax.fori_loop(0, peers, lap, start)


def contract(form, left, right):
    return jnp.einsum(form, left, right, precision=lax.Precision.HIGHEST)


def rotation(angle_index, period):
    angles = 2.0 * math.pi / period * angle_index.astype(jnp.float32)
    return (jnp.cos(angles), jnp.sin(angles))


def dft_tables(lon_count):
    inner_count = lon_count // 64
    coarse_index = jnp.arange(64, dtype=jnp.int32)
    fine_index = jnp.arange(inner_count, dtype=jnp.int32)
    mode_index = jnp.arange(inner_count // 2, dtype=jnp.int32)
    section_one = rotation(coarse_index[:, None] * coarse_index[None, :] % 64, 64)
    twiddle = rotation(coarse_index[:, None] * fine_index[None, :], lon_count)
    section_two = rotation(mode_index[:, None] * fine_index[None, :] % inner_count, inner_count)
    return (section_one, twiddle, section_two)


def forward_dft(grid):
    row_count, lon_count = grid.shape
    (cos_one, sin_one), (cos_tw, sin_tw), (cos_two, sin_two) = dft_tables(lon_count)
    lattice = grid.reshape(row_count, 64, lon_count // 64)
    real_a = contract("ab,rbc->rac", cos_one, lattice)
    imag_a = -contract("ab,rbc->rac", sin_one, lattice)
    real_b = real_a * cos_tw + imag_a * sin_tw
    imag_b = imag_a * cos_tw - real_a * sin_tw
    real_x = contract("rac,dc->rda", real_b, cos_two) + contract("rac,dc->rda", imag_b, sin_two)
    imag_x = contract("rac,dc->rda", imag_b, cos_two) - contract("rac,dc->rda", real_b, sin_two)
    wavenumbers = jnp.arange(lon_count // 2, dtype=jnp.int32).reshape(lon_count // 128, 64)
    weight = jnp.where(wavenumbers == 0, 1.0 / lon_count, 2.0 / lon_count).astype(jnp.float32)
    return jnp.stack([weight * real_x, -weight * imag_x], axis=-1).reshape(row_count, lon_count)


def inverse_dft(spectrum):
    row_count, lon_count = spectrum.shape
    (cos_one, sin_one), (cos_tw, sin_tw), (cos_two, sin_two) = dft_tables(lon_count)
    modes_pair = spectrum.reshape(row_count, lon_count // 128, 64, 2)
    real_z = modes_pair[..., 0]
    imag_z = -modes_pair[..., 1]
    real_p = contract("rda,dc->rac", real_z, cos_two) - contract("rda,dc->rac", imag_z, sin_two)
    imag_p = contract("rda,dc->rac", real_z, sin_two) + contract("rda,dc->rac", imag_z, cos_two)
    real_q = real_p * cos_tw - imag_p * sin_tw
    imag_q = real_p * sin_tw + imag_p * cos_tw
    lattice = contract("rac,ab->rbc", real_q, cos_one) - contract("rac,ab->rbc", imag_q, sin_one)
    return lattice.reshape(row_count, lon_count)


def spectral_slope(values, wavenumbers, lon_count):
    slope_factor = 2.0 * math.pi / lon_count * wavenumbers.astype(jnp.float32)
    return jnp.stack(
        [slope_factor[None, :] * values[..., 1], -slope_factor[None, :] * values[..., 0]], axis=-1
    )


def sweep_down(inverses, right_side, coupling, incoming):

    def advance(carried, inputs):
        inverse_block, values, coupling_value = inputs
        values = values.at[:, 0].add(-coupling_value * carried)
        product = jnp.einsum(
            "mpq,sqmc->spmc", inverse_block, values, precision=lax.Precision.HIGHEST
        )
        return (product[:, -1], product)

    outgoing, images = lax.scan(
        advance, incoming, (inverses, jnp.moveaxis(right_side, 1, 0), coupling)
    )
    return (jnp.moveaxis(images, 0, 1), outgoing)


def sweep_up(inverses, images, coupling, incoming):

    def advance(carried, inputs):
        inverse_block, values, coupling_value = inputs
        solved = values - jnp.einsum(
            "mp,smc->spmc", inverse_block[:, :, -1], carried, precision=lax.Precision.HIGHEST
        )
        return (coupling_value * solved[:, 0], solved)

    outgoing, solved = lax.scan(
        advance, incoming, (inverses, jnp.moveaxis(images, 1, 0), coupling), reverse=True
    )
    return (jnp.moveaxis(solved, 0, 1), outgoing)


def compose(earlier, later):
    return (later[0] + later[1] * earlier[0], later[1] * earlier[1])


def general_device(
    adjoint_u, adjoint_v, adjoint_h, zonal_wind, meridional_wind, block_inverse, coupling
):
    band_rows = adjoint_h.shape[0]
    band_count = lax.axis_size("lat")
    lat_total = band_rows * band_count
    first_row = lax.axis_index("lat") * band_rows
    row_index = (first_row + jnp.arange(band_rows, dtype=jnp.int32)).astype(jnp.float32)
    latitude = jnp.pi * (row_index + 0.5) / lat_total - 0.5 * jnp.pi
    stretch = 0.25 / (0.3 + jnp.cos(latitude))
    coriolis = 0.5 * jnp.sin(latitude)
    fields = jnp.stack([adjoint_u, adjoint_v, adjoint_h])
    zonal_flux = zonal_wind.astype(jnp.float32)[None] * fields
    meridional_flux = meridional_wind.astype(jnp.float32)[None] * fields
    zonal_pad = padded(zonal_flux, (("lon", 2),), 1, True)
    meridional_pad = padded(meridional_flux, (("lat", 1),), 1, False)
    result = fields - stretch[None, :, None] * (zonal_pad[:, :, :-2] - zonal_pad[:, :, 2:])
    result = result - meridional_rate * (meridional_pad[:, :-2] - meridional_pad[:, 2:])
    adj_u = result[0] - coriolis[:, None] * adjoint_v
    adj_v = result[1] + coriolis[:, None] * adjoint_u
    adj_h = result[2]
    row_layout = lax.all_to_all(adj_h, "lon", split_axis=0, concat_axis=1, tiled=True)
    lon_count = row_layout.shape[1]
    spectrum = lax.all_to_all(
        forward_dft(row_layout), "lon", split_axis=1, concat_axis=0, tiled=True
    )
    blocks = block_inverse.shape[0]
    owned_modes = block_inverse.shape[1]
    block_rows = P_SIZE
    inverses = block_inverse.reshape(blocks, owned_modes, block_rows, block_rows)
    right_side = spectrum.reshape(blocks, block_rows, owned_modes, 2)[None]
    nothing = jnp.zeros((1, owned_modes, 2), jnp.float32)
    start_pair = jnp.concatenate([nothing, nothing + 1.0])
    identity_map = (nothing[0], nothing[0] + 1.0)
    images, outgoing = sweep_down(
        inverses, jnp.concatenate([right_side, jnp.zeros_like(right_side)]), coupling, start_pair
    )
    prefix_map = entering((outgoing[0], outgoing[1]), "lat", compose, identity_map, False)
    images = images[:1] + images[1:] * prefix_map[0]
    solved, outgoing = sweep_up(
        inverses, jnp.concatenate([images, jnp.zeros_like(images)]), coupling, start_pair
    )
    prefix_map = entering((outgoing[0], outgoing[1]), "lat", compose, identity_map, True)
    solved = solved[0] + solved[1] * prefix_map[0]
    solved = solved.reshape(band_rows, owned_modes, 2)
    wavenumbers = lax.axis_index("lon") * owned_modes + jnp.arange(owned_modes, dtype=jnp.int32)
    slope = spectral_slope(solved, wavenumbers, lon_count)
    stacked = jnp.stack(
        [solved.reshape(band_rows, 2 * owned_modes), slope.reshape(band_rows, 2 * owned_modes)]
    )
    spectra = lax.all_to_all(stacked, "lon", split_axis=1, concat_axis=2, tiled=True)
    grids = inverse_dft(spectra.reshape(-1, lon_count)).reshape(2, -1, lon_count)
    local_grids = lax.all_to_all(grids, "lon", split_axis=2, concat_axis=1, tiled=True)
    out_u = adj_u + stretch[:, None] * local_grids[1]
    return (out_u, adj_v, local_grids[0])


LANES = 128
SUBLANES = 8
F32 = jnp.float32
BF16 = jnp.bfloat16


def split_table(table):
    high = np.asarray(table, np.float32).astype(BF16)
    low = (table - high.astype(np.float64)).astype(BF16)
    return np.concatenate([high, high, low], axis=-1)


def spectral_tables(lon_count):
    coarse = lon_count // LANES
    modes = coarse // 2
    b, c, a = (np.arange(LANES), np.arange(LANES), np.arange(coarse))
    owners = modes // 4
    d = (np.arange(owners)[:, None, None] * 4 + np.zeros((1, 2, 1), int) + np.arange(4)).reshape(-1)
    part = np.tile(np.repeat(np.arange(2), 4), owners)
    ba = 2 * np.pi * (np.outer(b, a) % coarse) / coarse
    dc = 2 * np.pi * (np.outer(d, c) % coarse) / coarse
    bc = 2 * np.pi * np.outer(b, c) / lon_count
    is_sine = part[:, None] == 1
    cos_dc, sin_dc = (np.cos(dc), np.sin(dc))
    forward_one = np.concatenate([np.cos(ba), -np.sin(ba)])
    forward_two = np.concatenate([np.where(is_sine, sin_dc, cos_dc), np.where(is_sine, -cos_dc, sin_dc)], 1)
    inverse_one = np.concatenate([np.where(is_sine, sin_dc, cos_dc).T, np.where(is_sine, -cos_dc, sin_dc).T])
    slope_one = np.concatenate([np.where(is_sine, cos_dc, -sin_dc).T, np.where(is_sine, sin_dc, cos_dc).T])
    inverse_two = np.concatenate([np.cos(ba).T, -np.sin(ba).T], 1)
    wavenumber = LANES * d[:, None] + b[None, :]
    weight = np.where(wavenumber == 0, 1.0, 2.0) / lon_count
    slope = 2 * np.pi / lon_count * wavenumber
    return {
        "forward_one": split_table(forward_one),
        "forward_two": split_table(forward_two),
        "inverse_one": split_table(inverse_one),
        "slope_one": split_table(slope_one),
        "inverse_two": split_table(inverse_two),
        "twiddle": np.stack([np.cos(bc), np.sin(bc)]).astype(np.float32),
        "weight": weight.astype(np.float32),
        "slope": slope.astype(np.float32),
    }


def band_tables(lat_total):
    latitude = np.pi * (np.arange(lat_total) + 0.5) / lat_total - 0.5 * np.pi
    stretch = 0.25 / (0.3 + np.cos(latitude))
    coriolis = 0.5 * np.sin(latitude)
    return (stretch.astype(np.float32)[:, None], coriolis.astype(np.float32)[:, None])


def halves(value):
    high = value.astype(BF16)
    return (high, (value - high.astype(F32)).astype(BF16))


def edges_kernel(*refs):
    fields, (zonal, meridional), outs = (refs[:3], refs[3:5], refs[5:])
    to_right, to_left, to_next, to_previous = outs
    rows, columns = fields[0].shape
    for out in outs:
        out[...] = jnp.zeros(out.shape, F32)
    for f, field in enumerate(fields):
        for out, at, line in ((to_right, columns - LANES, LANES - 1), (to_left, 0, 0)):
            flux = zonal[:, at : at + LANES].astype(F32) * field[:, at : at + LANES]
            out[f : f + 1, :] = flux.T[line : line + 1, :]
        for out, at, line in ((to_next, rows - 16, 15), (to_previous, 0, 0)):
            flux = meridional[at : at + 16, :].astype(F32) * field[at : at + 16, :]
            out[f : f + 1, :] = flux[line : line + 1, :]


def advected(f, field, zonal, meridional, from_left, from_right, from_previous, from_next, stretch):
    rows, columns = field.shape
    tiles = columns // LANES
    lane = lax.broadcasted_iota(jnp.int32, (rows, LANES), 1)
    row = lax.broadcasted_iota(jnp.int32, (rows, LANES), 0)
    outer = [
        jnp.broadcast_to(ref[f : f + 1, :], (LANES, rows)).T for ref in (from_left, from_right)
    ]
    wide = jnp.broadcast_to(stretch[...], (rows, LANES))

    def part(ref, k):
        return ref[:, k * LANES : (k + 1) * LANES].astype(F32)

    for k in range(tiles):
        here = part(field, k)
        flux = part(zonal, k) * here
        before = outer[0] if k == 0 else pltpu.roll(part(zonal, k - 1) * part(field, k - 1), 1, 1)
        after = (
            outer[1]
            if k == tiles - 1
            else pltpu.roll(part(zonal, k + 1) * part(field, k + 1), LANES - 1, 1)
        )
        west = jnp.where(lane == 0, before, pltpu.roll(flux, 1, 1))
        east = jnp.where(lane == LANES - 1, after, pltpu.roll(flux, LANES - 1, 1))
        flux = part(meridional, k) * here
        at = slice(k * LANES, (k + 1) * LANES)
        south = jnp.where(row == 0, from_previous[f : f + 1, at], pltpu.roll(flux, 1, 0))
        north = jnp.where(row == rows - 1, from_next[f : f + 1, at], pltpu.roll(flux, rows - 1, 0))
        yield (k, here - wide * (west - east) - meridional_rate * (south - north))


def depth_kernel(field, zonal, meridional, left, right, previous, next_, stretch, out):
    rows = field.shape[0]
    for k, tile in advected(2, field, zonal, meridional, left, right, previous, next_, stretch):
        out[pl.ds(k, rows, stride=SUBLANES), :] = tile


def wind_kernel(u, v, zonal, meridional, left, right, previous, next_, stretch, coriolis, out_u, out_v):
    turn = jnp.broadcast_to(coriolis[...], (u.shape[0], LANES))
    arguments = (zonal, meridional, left, right, previous, next_, stretch)
    for f, (field, other, out, sign) in enumerate(((u, v, out_u, -1.0), (v, u, out_v, 1.0))):
        for k, tile in advected(f, field, *arguments):
            at = slice(k * LANES, (k + 1) * LANES)
            out[:, at] = tile + sign * turn * other[:, at]


def product_nt(left, right):
    return lax.dot_general(left, right, (((1,), (1,)), ((), ())), preferred_element_type=F32)


def two_stage(rows_of, one, cos, sin, two):
    tiles = [halves(tile) for tile in rows_of]
    stacked = jnp.concatenate(
        [jnp.concatenate([high, low, high], axis=0) for high, low in tiles], axis=1
    )
    first = jnp.dot(one, stacked, preferred_element_type=F32)
    rotated = []
    for k in range(len(tiles)):
        real = first[:LANES, k * LANES : (k + 1) * LANES]
        imag = first[LANES:, k * LANES : (k + 1) * LANES]
        turned = jnp.concatenate([real * cos - imag * sin, real * sin + imag * cos], axis=1)
        high, low = halves(turned)
        rotated.append(jnp.concatenate([high, low, high], axis=1))
    return product_nt(two, jnp.concatenate(rotated, axis=0))


def forward_kernel(grid, one, twiddle, two, weight, out):
    owners, rows = grid.shape[:2]
    cos, sin = (twiddle[0], -twiddle[1])
    for r in range(0, rows, 2):
        tiles = [grid[:, r + k].reshape(owners * SUBLANES, LANES) for k in range(2)]
        modes = two_stage(tiles, one[...], cos, sin, two[...])
        for k in range(2):
            scaled = weight[...] * modes[:, k * LANES : (k + 1) * LANES]
            out[:, r + k] = scaled.reshape(owners, SUBLANES, LANES)


def inverse_kernel(spectrum, one, slope_one, twiddle, two, slope, out):
    owners, rows = spectrum.shape[:2]
    cos, sin = (twiddle[0], twiddle[1])
    for r in range(0, rows, 2):
        tiles = [spectrum[:, r + k].reshape(owners * SUBLANES, LANES) for k in range(2)]
        for f, table in enumerate((one, slope_one)):
            if f:
                tiles = [slope[...] * tile for tile in tiles]
            lons = two_stage(tiles, table[...], cos, sin, two[...])
            for k in range(2):
                out[:, f, r + k] = lons[:, k * LANES : (k + 1) * LANES].reshape(
                    owners, SUBLANES, LANES
                )


def blocks_kernel(coupling, given, turned, first_column, last_column, maps):
    block, blocks = (pl.program_id(0), pl.num_programs(0))
    size = P_SIZE
    half = SUBLANES // 2
    for group in range(half):
        for side in range(size * size // LANES):
            entries = given[0, group * LANES : (group + 1) * LANES, side * LANES : (side + 1) * LANES].T
            for part in range(2):
                start = side * LANES * SUBLANES + part * half + group
                turned[0, pl.ds(start, LANES, stride=SUBLANES), :] = entries
    for p in range(size):
        start = p * size * SUBLANES
        first_column[block, p] = turned[0, start : start + SUBLANES, :]
        start += (size - 1) * SUBLANES
        last_column[block, p] = turned[0, start : start + SUBLANES, :]

    @pl.when(block == blocks - 1)
    def _():
        count = first_column.shape[0]
        one = jnp.ones((SUBLANES, LANES), F32)
        carried = [one]
        for b in range(count):
            carried.append(-coupling[b] * first_column[b, size - 1] * carried[b])
        forward, back = (jnp.zeros_like(one), one)
        for b in reversed(range(count)):
            forward = coupling[b] * (
                -coupling[b] * first_column[b, 0] * carried[b] - last_column[b, 0] * forward
            )
            back = -coupling[b] * last_column[b, 0] * back
        maps[0] = carried[count]
        maps[1] = forward
        maps[2] = back


def images_kernel(coupling, values, turned, images, offsets, middle, ends):
    block, blocks = (pl.program_id(0), pl.num_programs(0))
    size = P_SIZE

    @pl.when(block == 0)
    def _():
        offsets[...] = jnp.zeros(offsets.shape, F32)

    given = [values[0, q] for q in range(size)]
    for p in range(size):
        total = turned[0, p * size] * given[0]
        for q in range(1, size):
            total += turned[0, p * size + q] * given[q]
        images[0, p] = total
    entering_value = coupling[block] * offsets[0]
    middle[block] = images[0, 0] - entering_value * turned[0, 0]
    ends[block] = turned[0, size - 1]
    offsets[0] = images[0, size - 1] - entering_value * turned[0, (size - 1) * size]

    @pl.when(block == blocks - 1)
    def _():
        count = middle.shape[0]
        back = jnp.zeros((SUBLANES, LANES), F32)
        for b in reversed(range(count)):
            back = coupling[b] * (middle[b] - ends[b] * back)
        offsets[1] = back


def solved_kernel(place, coupling, images, first_column, last_column, *refs):
    count = len(refs) // 2 - 1
    maps, offsets, out, bands, carried = (
        refs[:count],
        refs[count : 2 * count],
        refs[2 * count],
        refs[2 * count + 1],
        refs[2 * count + 2],
    )
    mine = place[0]
    for k in range(count):
        band = lax.rem(mine + k, count)
        bands[band, 0:3] = maps[k][...]
        bands[band, 3:5] = offsets[k][...]
    zero = jnp.zeros((SUBLANES, LANES), F32)
    rising = [zero]
    for k in range(count - 1):
        rising.append(bands[k, 3] + bands[k, 0] * rising[k])
    falling = zero
    carried[count - 1, 1] = falling
    for k in reversed(range(1, count)):
        falling = bands[k, 4] + bands[k, 1] * rising[k] + bands[k, 2] * falling
        carried[k - 1, 1] = falling
    for k in range(count):
        carried[k, 0] = rising[k]
    size = P_SIZE
    blocks = images.shape[0]
    below = [coupling[0] * carried[mine, 0]]
    for b in range(blocks - 1):
        last = images[b, size - 1] - below[b] * first_column[b, size - 1]
        below.append(coupling[b + 1] * last)
    above = carried[mine, 1]
    for b in reversed(range(blocks)):
        for p in range(size):
            out[b, p] = images[b, p] - below[b] * first_column[b, p] - above * last_column[b, p]
        above = coupling[b] * out[b, 0]


def final_kernel(grids, adj_u, stretch, out_u, out_h):
    rows = adj_u.shape[0]
    tiles = adj_u.shape[1] // LANES
    sources = grids.shape[0] // (2 * P_SIZE * SUBLANES)
    for q in range(sources):
        for g in range(0, P_SIZE, SUBLANES):
            at = slice(q * P_SIZE + g, q * P_SIZE + g + SUBLANES)
            wide = jnp.broadcast_to(stretch[at, :], (SUBLANES, LANES))
            for k in range(tiles):
                lons = slice(k * LANES, (k + 1) * LANES)
                start = (2 * q * P_SIZE + g) * SUBLANES + k
                out_h[at, lons] = grids[pl.ds(start, SUBLANES, stride=SUBLANES), :]
                start += P_SIZE * SUBLANES
                gradient = grids[pl.ds(start, SUBLANES, stride=SUBLANES), :]
                out_u[at, lons] = adj_u[at, lons] + wide * gradient


def shape_of(*dims):
    return jax.ShapeDtypeStruct(dims, F32)


VMEM = pl.BlockSpec(memory_space=pltpu.VMEM)
SMEM = pl.BlockSpec(memory_space=pltpu.SMEM)


def call(kernel, name, outs, *args, smem=0, grid=None, in_specs=None, out_specs=None, scratch=(), limit=16, flops=0):
    moved = sum(4 * math.prod(leaf.shape) for leaf in (*args, *outs))
    return pl.pallas_call(
        kernel,
        name=name,
        out_shape=outs,
        in_specs=in_specs or [SMEM] * smem + [VMEM] * (len(args) - smem),
        out_specs=out_specs or [VMEM] * len(outs),
        scratch_shapes=scratch,
        compiler_params=pltpu.CompilerParams(vmem_limit_bytes=limit << 20),
        cost_estimate=pl.CostEstimate(flops=flops, bytes_accessed=moved, transcendentals=0),
        **({"grid": grid} if grid else {}),
    )(*args)


def transposed(blocks):
    return lax.all_to_all(blocks, "lon", split_axis=0, concat_axis=0, tiled=True)


def around(value, axis):
    count = lax.axis_size(axis)
    return [value] + [
        lax.ppermute(value, axis, [((i + k) % count, i) for i in range(count)])
        for k in range(1, count)
    ]


def tiled_device(u, v, h, zonal, meridional, block_inverse, coupling):
    rows, columns = h.shape
    lon_size, lat_size = (lax.axis_size("lon"), lax.axis_size("lat"))
    lon_count = columns * lon_size
    blocks, owned, entries = block_inverse.shape
    table = spectral_tables(lon_count)
    place = lax.axis_index("lat").reshape(1)
    stretch, coriolis = (
        lax.dynamic_slice_in_dim(jnp.asarray(t), lax.axis_index("lat") * rows, rows)
        for t in band_tables(rows * lat_size)
    )
    tile = (SUBLANES, LANES)
    lon_edge, lat_edge = (shape_of(SUBLANES, rows), shape_of(SUBLANES, columns))
    edges = call(edges_kernel, "edges", [lon_edge, lon_edge, lat_edge, lat_edge], u, v, h, zonal, meridional)
    ring = [(i, (i + 1) % lon_size) for i in range(lon_size)]
    line = [(i, i + 1) for i in range(lat_size - 1)]
    halo = (
        lax.ppermute(edges[0], "lon", ring),
        lax.ppermute(edges[1], "lon", [(j, i) for i, j in ring]),
        lax.ppermute(edges[2], "lat", line),
        lax.ppermute(edges[3], "lat", [(j, i) for i, j in line]),
    )
    turned, first_column, last_column, maps = call(
        blocks_kernel,
        "blocks",
        [
            shape_of(blocks, entries * SUBLANES, LANES),
            shape_of(blocks, P_SIZE, *tile),
            shape_of(blocks, P_SIZE, *tile),
            shape_of(3, *tile),
        ],
        coupling,
        block_inverse,
        grid=(blocks,),
        in_specs=[SMEM, pl.BlockSpec((1, owned, entries), lambda b: (b, 0, 0))],
        out_specs=[
            pl.BlockSpec((1, entries * SUBLANES, LANES), lambda b: (b, 0, 0)),
            pl.BlockSpec((blocks, P_SIZE, *tile), lambda b: (0, 0, 0, 0)),
            pl.BlockSpec((blocks, P_SIZE, *tile), lambda b: (0, 0, 0, 0)),
            pl.BlockSpec((3, *tile), lambda b: (0, 0, 0)),
        ],
    )
    (spread,) = call(depth_kernel, "depth", [shape_of(rows * SUBLANES, LANES)], h, zonal, meridional, *halo, stretch)
    all_maps = around(maps, "lat")
    lattice = transposed(spread.reshape(lon_size, P_SIZE, *tile))
    adj_u, adj_v = call(
        wind_kernel, "wind", [shape_of(rows, columns)] * 2, u, v, zonal, meridional, *halo, stretch, coriolis
    )
    (spectrum,) = call(
        forward_kernel,
        "forward",
        [shape_of(lon_size, P_SIZE, *tile)],
        lattice,
        *(jnp.asarray(table[key]) for key in ("forward_one", "twiddle", "forward_two", "weight")),
    )
    values = transposed(spectrum)
    images, offsets = call(
        images_kernel,
        "images",
        [shape_of(blocks, P_SIZE, *tile), shape_of(2, *tile)],
        coupling,
        values,
        turned.reshape(blocks, entries, *tile),
        grid=(blocks,),
        in_specs=[
            SMEM,
            pl.BlockSpec((1, P_SIZE, *tile), lambda b: (b, 0, 0, 0)),
            pl.BlockSpec((1, entries, *tile), lambda b: (b, 0, 0, 0)),
        ],
        out_specs=[
            pl.BlockSpec((1, P_SIZE, *tile), lambda b: (b, 0, 0, 0)),
            pl.BlockSpec((2, *tile), lambda b: (0, 0, 0)),
        ],
        scratch=[pltpu.VMEM((blocks, *tile), F32)] * 2,
    )
    all_offsets = around(offsets, "lat")
    (solved,) = call(
        solved_kernel,
        "solved",
        [shape_of(blocks, P_SIZE, *tile)],
        place,
        coupling,
        images,
        first_column,
        last_column,
        *all_maps,
        *all_offsets,
        smem=2,
        scratch=[pltpu.VMEM((lat_size, 5, *tile), F32), pltpu.VMEM((lat_size, 2, *tile), F32)],
    )
    spectra = transposed(solved)
    (grids,) = call(
        inverse_kernel,
        "inverse",
        [shape_of(lon_size, 2, P_SIZE, *tile)],
        spectra,
        *(jnp.asarray(table[key]) for key in ("inverse_one", "slope_one", "twiddle", "inverse_two", "slope")),
    )
    local = transposed(grids)
    out_u, out_h = call(
        final_kernel,
        "final",
        [shape_of(rows, columns)] * 2,
        local.reshape(-1, LANES),
        adj_u,
        stretch,
    )
    return (out_u, adj_v, out_h)


def per_device(*args):
    rows, columns = args[2].shape
    tiles = columns == SUBLANES * LANES and rows == P_SIZE * lax.axis_size("lon")
    return (tiled_device if tiles and rows == LANES else general_device)(*args)


def solution(mesh):
    return jax.shard_map(
        per_device,
        mesh=mesh,
        in_specs=(
            P("lat", "lon"),
            P("lat", "lon"),
            P("lat", "lon"),
            P("lat", "lon"),
            P("lat", "lon"),
            P("lat", "lon", None),
            P("lat"),
        ),
        out_specs=(P("lat", "lon"), P("lat", "lon"), P("lat", "lon")),
        check_vma=False,
    )
```
